32 devices in a mesh: seq: 8 (over z, x), chan: 4 (over y, core).
Axes of the slice: x: 2, y: 2, z: 4, core: 2. Of those that a mesh axis runs over, the one named last changes fastest.
Arguments:
- signal: float32 [256, 65536], P('chan', 'seq'), may hold values from -6 to 6
- gating: float32 [256, 65536], P('chan', 'seq'), may hold values from -6 to 6
- response: float32 [256, 65536], P('chan', 'seq'), may hold values from -0.0234375 to 0.0234375
- skip_gain: float32 [256], P('chan'), may hold values from -4 to 4
- mixing_weight: float32 [256, 256], P(None, 'chan'), may hold values from -0.5 to 0.5
Outputs:
- output: float32 [256, 65536], P('chan', 'seq')
The draws below stay inside these ranges and needn't reach their ends.
All inputs are finite; a program needn't handle non-finite values.
Results may differ from the reference program's by a relative error of at most 0.00007.
Values sent between devices are 32-bit elements; how exact they have to be, the bound alone decides.
A program may use at most 128 MiB of HBM per device.

```python
import jax
import jax.numpy as jnp
from jax import lax

D = 256
LENGTH = 65536


def with_spikes(values, own_key, source, target, parts, factor):
    def block_of(position):
        return (jnp.arange(values.shape[position]) // (values.shape[position] // parts)).reshape((-1,) + (1,) * (values.ndim - 1 - position))

    first = jax.random.permutation(own_key, parts)[block_of(target)]
    second = (block_of(target) + parts // 2) % parts
    return jnp.where((block_of(source) == first) | (block_of(source) == second), factor * values, values)


def steps_of(stream_key, shape, shards, least, high):
    loudness = 1.0
    for position, shards_of in shards:
        heights = jax.random.uniform(jax.random.fold_in(jax.random.fold_in(stream_key, 6), position), (shards_of,), jnp.float32, least / len(shards), high / len(shards))
        loudness = loudness * jnp.repeat(jnp.exp(heights), shape[position] // shards_of).reshape((-1,) + (1,) * (len(shape) - 1 - position))
    return loudness


def scatter_about(rng, shape, spread, reach, pieces=(), kind=jnp.bfloat16):
    values = jax.random.normal(rng, shape, jnp.float32) * spread
    if len(pieces) > 0:
        values = steps_of(rng, shape, pieces, -0.22, 0.18) * values
    return jnp.clip(values, min=-reach, max=reach).astype(kind)


def gaussian_with(rng, shape, deviation, most, split, heavy, kind=jnp.bfloat16):
    entries = deviation * jax.random.normal(rng, shape, jnp.float32)
    if split:
        entries = entries * steps_of(rng, shape, split, -0.22, 0.18)
    return jnp.clip(with_spikes(entries, jax.random.fold_in(rng, 3), *heavy), -most, most).astype(kind)


def setup_inputs(seed: int = 0) -> dict:
    keys = jax.random.split(jax.random.key(seed), 6)
    return {
        "signal": scatter_about(keys[0], (D, LENGTH), 1.0, 6.0, ((0, 4), (1, 8)), jnp.float32),
        "gating": scatter_about(keys[1], (D, LENGTH), 1.0, 6.0, ((0, 4), (1, 8)), jnp.float32),
        "response": scatter_about(keys[2], (D, LENGTH), LENGTH ** -0.5, 0.0234375, ((0, 4), (1, 8)), jnp.float32),
        "skip_gain": scatter_about(keys[3], (D,), 1.0, 4.0, ((0, 4),), jnp.float32),
        "mixing_weight": gaussian_with(keys[4], (D, D), D ** -0.5, 0.5, ((1, 4),), (1, 0, 4, 2.0), jnp.float32),
    }


def reference(signal, gating, response, skip_gain, mixing_weight):
    span = signal.shape[1]
    signal_spec = jnp.fft.rfft(signal, n=2 * span, axis=1)
    response_spec = jnp.fft.rfft(response, n=2 * span, axis=1)
    conv = jnp.fft.irfft(signal_spec * response_spec, n=2 * span, axis=1)[:, :span].astype(signal.dtype)
    mixed_in = gating * (conv + skip_gain[:, None] * signal)
    return jnp.dot(mixing_weight, mixed_in, precision=lax.Precision.HIGHEST, preferred_element_type=jnp.float32)
```

```python
from functools import partial
import math

import jax
import jax.numpy as jnp
import numpy as np
from jax import lax
from jax.experimental import pallas as pl
from jax.experimental.pallas import tpu as pltpu
from jax.sharding import PartitionSpec as P

INNER = 256


def halves(table):
    high = np.asarray(table, np.float32).astype(jnp.bfloat16)
    low = (np.asarray(table, np.float64) - high.astype(np.float64)).astype(np.float32).astype(jnp.bfloat16)
    return high, low


def split(value):
    high = value.astype(jnp.bfloat16)
    return high, (value - high.astype(jnp.float32)).astype(jnp.bfloat16)


def tables(span):
    outer = span // INNER
    step_out = np.arange(outer, dtype=np.float64)
    step_in = np.arange(INNER, dtype=np.float64)
    angle = 2 * np.pi * np.mod((4 * step_out[:, None] + 1) * step_out[None, :], 4 * outer) / (4 * outer)
    cos_out, sin_out = np.cos(angle), -np.sin(angle)
    high, low = halves(np.concatenate([cos_out, sin_out], axis=0))
    first = np.concatenate([high, high, low], axis=1)
    angle = 2 * np.pi * np.mod((4 * step_out[:, None] + 1) * step_in[None, :], 4 * span) / (4 * span)
    twiddle = np.stack([np.cos(angle), -np.sin(angle)]).astype(np.float32)
    angle = 2 * np.pi * np.mod(step_in[:, None] * step_in[None, :], INNER) / INNER
    cos_in, sin_in = np.cos(angle), -np.sin(angle)
    high, low = halves(np.block([[cos_in, sin_in], [-sin_in, cos_in]]))
    second = np.concatenate([high, high, low], axis=0)
    high, low = halves(np.block([[cos_in, -sin_in], [sin_in, cos_in]]))
    third = np.concatenate([high, high, low], axis=0)
    high, low = halves(np.concatenate([cos_out.T, sin_out.T], axis=1) / span)
    fourth = np.concatenate([high, high, low], axis=1)
    return first, twiddle, second, third, fourth


def matmul(left, right):
    return jnp.dot(left, right, preferred_element_type=jnp.float32)


def conv_row(signal, response, first, twiddle, second, third, fourth):
    outer = signal.shape[0]
    high, low = split(jnp.concatenate([signal, response], axis=1))
    mid = matmul(first[...], jnp.concatenate([high, low, high], axis=0))
    tw_real, tw_imag = twiddle[0], twiddle[1]
    spectra = []
    for place in range(2):
        cols = slice(place * INNER, (place + 1) * INNER)
        real, imag = mid[:outer, cols], mid[outer:, cols]
        turned = jnp.concatenate(
            [real * tw_real - imag * tw_imag, real * tw_imag + imag * tw_real], axis=1
        )
        high, low = split(turned)
        spectra.append(matmul(jnp.concatenate([high, low, high], axis=1), second[...]))
    s_real, s_imag = spectra[0][:, :INNER], spectra[0][:, INNER:]
    r_real, r_imag = spectra[1][:, :INNER], spectra[1][:, INNER:]
    prod = jnp.concatenate(
        [s_real * r_real - s_imag * r_imag, s_real * r_imag + s_imag * r_real], axis=1
    )
    high, low = split(prod)
    back = matmul(jnp.concatenate([high, low, high], axis=1), third[...])
    real, imag = back[:, :INNER], back[:, INNER:]
    turned = jnp.concatenate(
        [real * tw_real + imag * tw_imag, imag * tw_real - real * tw_imag], axis=0
    )
    high, low = split(turned)
    return matmul(fourth[...], jnp.concatenate([high, low, high], axis=0))


def conv_kernel(rows_ref, first, twiddle, second, third, fourth, out_ref):
    out_ref[0] = conv_row(rows_ref[0, 0], rows_ref[1, 0], first, twiddle, second, third, fourth)


def conv_call(rows):
    own_rows, outer, inner = rows.shape[1:]
    consts = [jnp.asarray(t) for t in tables(outer * inner)]
    whole = pl.BlockSpec(memory_space=pltpu.VMEM)
    return pl.pallas_call(
        conv_kernel,
        grid=(own_rows,),
        in_specs=[pl.BlockSpec((2, 1, outer, inner), lambda r: (0, r, 0, 0))] + [whole] * 5,
        out_specs=pl.BlockSpec((1, outer, inner), lambda r: (r, 0, 0)),
        out_shape=jax.ShapeDtypeStruct((own_rows, outer, inner), jnp.float32),
        compiler_params=pltpu.CompilerParams(vmem_limit_bytes=60 * 2**20),
        name="conv",
    )(rows, *consts)


def per_device(signal, gating, response, skip_gain, mixing_weight):
    chan_rows, samples = signal.shape
    groups = lax.axis_size("seq")
    own_rows = chan_rows // groups
    outer = groups * samples // INNER
    stacked = jnp.stack([signal, response]).reshape(2, groups, own_rows, samples // INNER, INNER)
    rows = lax.all_to_all(stacked, "seq", split_axis=1, concat_axis=3, tiled=True)
    conv = conv_call(rows.reshape(2, own_rows, outer, INNER))
    conv = lax.all_to_all(
        conv.reshape(own_rows, groups, samples // INNER, INNER), "seq", split_axis=1, concat_axis=0, tiled=True
    ).reshape(chan_rows, samples)
    mixed_in = gating * (conv + skip_gain[:, None] * signal)
    return lax.psum_scatter(
        jnp.dot(
            mixing_weight,
            mixed_in,
            precision=lax.Precision.HIGHEST,
            preferred_element_type=jnp.float32,
        ),
        "chan",
        scatter_dimension=0,
        tiled=True,
    )


def solution(mesh):
    in_specs = (P("chan", "seq"), P("chan", "seq"), P("chan", "seq"), P("chan"), P(None, "chan"))
    out_specs = P("chan", "seq")
    return jax.shard_map(
        per_device, mesh=mesh, in_specs=in_specs, out_specs=out_specs, check_vma=False
    )
```

```python
from functools import partial
import math

import jax
import jax.numpy as jnp
import numpy as np
from jax import lax
from jax.experimental import pallas as pl
from jax.experimental.pallas import tpu as pltpu
from jax.sharding import PartitionSpec as P

INNER = 256


def halves(table):
    high = np.asarray(table, np.float32).astype(jnp.bfloat16)
    low = (np.asarray(table, np.float64) - high.astype(np.float64)).astype(np.float32).astype(jnp.bfloat16)
    return high, low


def split(value):
    high = value.astype(jnp.bfloat16)
    return high, (value - high.astype(jnp.float32)).astype(jnp.bfloat16)


def tables(span):
    outer = span // INNER
    step_out = np.arange(outer, dtype=np.float64)
    step_in = np.arange(INNER, dtype=np.float64)
    angle = 2 * np.pi * np.mod((4 * step_out[:, None] + 1) * step_out[None, :], 4 * outer) / (4 * outer)
    cos_out, sin_out = np.cos(angle), -np.sin(angle)
    first = np.concatenate(halves(np.concatenate([cos_out, sin_out], axis=0)), axis=1)
    angle = 2 * np.pi * np.mod((4 * step_out[:, None] + 1) * step_in[None, :], 4 * span) / (4 * span)
    twiddle = np.stack([np.cos(angle), -np.sin(angle)]).astype(np.float32)
    angle = 2 * np.pi * np.mod(step_in[:, None] * step_in[None, :], INNER) / INNER
    cos_in, sin_in = np.cos(angle), -np.sin(angle)
    second = np.concatenate(halves(np.block([[cos_in, sin_in], [-sin_in, cos_in]])), axis=0)
    last = np.concatenate(halves(np.concatenate([cos_out.T, -sin_out.T], axis=1) / span), axis=1)
    return first, twiddle, second, last


def matmul(left, right):
    return jnp.dot(left, right, preferred_element_type=jnp.float32)


def table_left(table, value):
    high, low = split(value)
    depth = value.shape[0]
    return matmul(table[...], jnp.concatenate([high, high], axis=0)) + matmul(table[:, :depth], low)


def table_right(value, table):
    high, low = split(value)
    depth = value.shape[1]
    return matmul(jnp.concatenate([high, high], axis=1), table[...]) + matmul(low, table[:depth, :])


def conv_row(signal, response, first, twiddle, second, last):
    outer = signal.shape[0]
    mid = table_left(first, jnp.concatenate([signal, response], axis=1))
    tw_real, tw_imag = twiddle[0], twiddle[1]
    turned = []
    for place in range(2):
        cols = slice(place * INNER, (place + 1) * INNER)
        real, imag = mid[:outer, cols], mid[outer:, cols]
        turned.append(jnp.concatenate(
            [real * tw_real - imag * tw_imag, real * tw_imag + imag * tw_real], axis=1
        ))
    spectra = table_right(jnp.concatenate(turned, axis=0), second)
    s_real, s_imag = spectra[:outer, :INNER], spectra[:outer, INNER:]
    r_real, r_imag = spectra[outer:, :INNER], spectra[outer:, INNER:]
    prod = jnp.concatenate(
        [s_real * r_real - s_imag * r_imag, -(s_real * r_imag + s_imag * r_real)], axis=1
    )
    back = table_right(prod, second)
    real, imag = back[:, :INNER], back[:, INNER:]
    turned = jnp.concatenate(
        [real * tw_real - imag * tw_imag, imag * tw_real + real * tw_imag], axis=0
    )
    return table_left(last, turned)


MESH_ID = pl.DeviceIdType.MESH


def layer_kernel(
    groups, own_rows, chans, signal, response, gating, skip, weight,
    first, twiddle, second, last, out,
    send, held, made, conv, mixed, wbuf,
    fwd_send, fwd_recv, back_send, back_recv, own_sem, row_send, row_recv, w_send, w_recv, sib_sem, sib_recv, rel_send, rel_recv,
):
    chan_rows = groups * own_rows
    samples = signal.shape[0] * 128 // chan_rows
    pieces = samples // INNER
    chips = chans // 2
    me = lax.axis_index("seq")
    mine = lax.axis_index("chan")
    chip, core = mine // 2, mine % 2
    sibling = chip * 2 + 1 - core
    out_rows = out.shape[0]

    barrier = pltpu.get_barrier_semaphore()
    for off in range(1, groups):
        pl.semaphore_signal(barrier, inc=1, device_id={"seq": lax.rem(me + off, groups)}, device_id_type=MESH_ID)
    for off in range(1, chans):
        pl.semaphore_signal(barrier, inc=1, device_id={"chan": lax.rem(mine + off, chans)}, device_id_type=MESH_ID)
    pl.semaphore_wait(barrier, groups + chans - 2)

    def native(ref, row, half):
        start = (row // 8) * (samples // 128 * 8) + lax.rem(row, 8) + 8 * half
        return ref[pl.ds(start, pieces, stride=16), :]

    def forward(j, off):
        peer = lax.rem(me + off, groups)
        return pltpu.make_async_remote_copy(
            send.at[j, peer], held.at[j, me], fwd_send.at[j, off - 1], fwd_recv.at[j, off - 1],
            device_id={"seq": peer}, device_id_type=MESH_ID)

    def backward(j, off):
        peer = lax.rem(me + off, groups)
        return pltpu.make_async_remote_copy(
            made.at[j, peer], conv.at[j, me], back_send.at[j, off - 1], back_recv.at[j, off - 1],
            device_id={"seq": peer}, device_id_type=MESH_ID)

    def own_in(j):
        return pltpu.make_async_copy(send.at[j, me], held.at[j, me], own_sem.at[0, j])

    def own_back(j):
        return pltpu.make_async_copy(made.at[j, me], conv.at[j, me], own_sem.at[1, j])

    block = groups * pieces

    def chunk(who, j):
        return mixed.at[:, pl.ds(pl.multiple_of((who * own_rows + j) * block, block), block), :]

    def to_sibling(j):
        return pltpu.make_async_remote_copy(
            chunk(mine, j), chunk(mine, j), sib_sem.at[j], sib_recv.at[j],
            device_id={"chan": sibling}, device_id_type=MESH_ID)

    def to_chip(j, off):
        return pltpu.make_async_remote_copy(
            chunk(mine, j), chunk(mine, j), row_send.at[j, off - 1], row_recv.at[j, off - 1],
            device_id={"chan": lax.rem(chip + off, chips) * 2 + core}, device_id_type=MESH_ID)

    def relay(j, off):
        who = lax.rem(chip + chips - off, chips) * 2 + core
        return pltpu.make_async_remote_copy(
            chunk(who, j), chunk(who, j), rel_send.at[j, off - 1], rel_recv.at[j, off - 1],
            device_id={"chan": sibling}, device_id_type=MESH_ID)

    def weights(off):
        peer = lax.rem(mine + off, chans)
        return pltpu.make_async_remote_copy(
            weight.at[pl.ds(pl.multiple_of(peer * out_rows, 8), out_rows), :], wbuf.at[off - 1],
            w_send.at[off - 1], w_recv.at[off - 1],
            device_id={"chan": peer}, device_id_type=MESH_ID)

    @pl.loop(0, own_rows)
    def _(j):
        for g in range(groups):
            for place, ref in enumerate((signal, response)):
                for half in range(2):
                    send[j, g, place, :, half * 128:(half + 1) * 128] = native(ref, g * own_rows + j, half)
        for off in range(1, groups):
            forward(j, off).start()
        own_in(j).start()

    for off in range(1, chans):
        weights(off).start()

    @pl.loop(0, own_rows)
    def _(j):
        own_in(j).wait()
        for off in range(1, groups):
            forward(j, off).wait_recv()
        rows = held[j]
        made[j] = conv_row(
            rows[:, 0].reshape(groups * pieces, INNER), rows[:, 1].reshape(groups * pieces, INNER),
            first, twiddle, second, last,
        ).reshape(groups, pieces, INNER)
        for off in range(1, groups):
            backward(j, off).start()
        own_back(j).start()

    def pass_on(j):
        for off in range(1, chips):
            to_chip(j, off).wait_recv()
            relay(j, off).start()

    @pl.loop(0, own_rows)
    def _(j):
        own_back(j).wait()
        for off in range(1, groups):
            backward(j, off).wait_recv()
        for g in range(groups):
            row = g * own_rows + j
            gain = skip[j, g:g + 1, :]
            for half in range(2):
                lanes = slice(half * 128, (half + 1) * 128)
                start = pl.multiple_of((mine * own_rows + j) * block + g * pieces, pieces)
                mixed[half, pl.ds(start, pieces), :] = native(gating, row, half) * (
                    conv[j, g, :, lanes] + gain * native(signal, row, half)
                )
        to_sibling(j).start()
        for off in range(1, chips):
            to_chip(j, off).start()

        @pl.when(j > 0)
        def _():
            pass_on(j - 1)

    pass_on(own_rows - 1)

    total = weight[pl.ds(pl.multiple_of(mine * out_rows, 8), out_rows), :]
    for off in range(1, chans):
        weights(off).wait()
        total = total + wbuf[off - 1]
    w_high, w_low = split(total)

    @pl.loop(0, own_rows)
    def _(j):
        for off in range(1, groups):
            forward(j, off).wait_send()
            backward(j, off).wait_send()
        to_sibling(j).wait()
        for off in range(1, chips):
            to_chip(j, off).wait_send()
            relay(j, off).wait()

    depth = chans * chan_rows

    @pl.loop(0, pieces)
    def _(i):
        for half in range(2):
            high, low = split(mixed[half, pl.ds(i, depth, stride=pieces), :])
            out[:, pl.ds(pl.multiple_of(i * INNER + half * 128, 128), 128)] = (
                matmul(w_high, high) + matmul(w_high, low) + matmul(w_low, high)
            )


def tiles(value):
    rows, columns = value.shape
    return value.reshape(rows // 8, 8, columns // 128, 128).transpose(0, 2, 1, 3).reshape(-1, 128)


def per_device(signal, gating, response, skip_gain, mixing_weight):
    chan_rows, samples = signal.shape
    groups = lax.axis_size("seq")
    chans = lax.axis_size("chan")
    own_rows = chan_rows // groups
    pieces = samples // INNER
    chips = chans // 2
    depth = mixing_weight.shape[0]
    out_rows = depth // chans
    consts = [jnp.asarray(t) for t in tables(groups * samples)]
    skip = jnp.broadcast_to(skip_gain.reshape(groups, own_rows).T[:, :, None], (own_rows, groups, 128))
    turned = mixing_weight.reshape(depth, groups, own_rows).swapaxes(1, 2).reshape(depth, chan_rows)
    weight = lax.dynamic_update_slice(
        jnp.zeros((depth, chans * chan_rows), jnp.float32), turned, (0, lax.axis_index("chan") * chan_rows)
    )
    whole = pl.BlockSpec(memory_space=pltpu.VMEM)
    f32 = jnp.float32
    sems = pltpu.SemaphoreType.DMA
    rows = chans * chan_rows * pieces
    return pl.pallas_call(
        partial(layer_kernel, groups, own_rows, chans),
        in_specs=[whole] * 9,
        out_specs=whole,
        out_shape=jax.ShapeDtypeStruct((out_rows, samples), f32),
        scratch_shapes=[
            pltpu.VMEM((own_rows, groups, 2, pieces, INNER), f32),
            pltpu.VMEM((own_rows, groups, 2, pieces, INNER), f32),
            pltpu.VMEM((own_rows, groups, pieces, INNER), f32),
            pltpu.VMEM((own_rows, groups, pieces, INNER), f32),
            pltpu.VMEM((2, rows, 128), f32),
            pltpu.VMEM((chans - 1, out_rows, chans * chan_rows), f32),
            sems((own_rows, groups - 1)), sems((own_rows, groups - 1)),
            sems((own_rows, groups - 1)), sems((own_rows, groups - 1)),
            sems((2, own_rows)),
            sems((own_rows, chips - 1)), sems((own_rows, chips - 1)),
            sems((chans - 1,)), sems((chans - 1,)),
            sems((own_rows,)), sems((own_rows,)),
            sems((own_rows, chips - 1)), sems((own_rows, chips - 1)),
        ],
        compiler_params=pltpu.CompilerParams(
            collective_id=0, has_side_effects=True, vmem_limit_bytes=62 * 2**20
        ),
        name="layer",
    )(tiles(signal), tiles(response), tiles(gating), skip, weight, *consts)


def solution(mesh):
    in_specs = (P("chan", "seq"), P("chan", "seq"), P("chan", "seq"), P("chan"), P(None, "chan"))
    out_specs = P("chan", "seq")
    return jax.shard_map(
        per_device, mesh=mesh, in_specs=in_specs, out_specs=out_specs, check_vma=False
    )
```

```python
from functools import partial
import math

import jax
import jax.numpy as jnp
import numpy as np
from jax import lax
from jax.experimental import pallas as pl
from jax.experimental.pallas import tpu as pltpu
from jax.sharding import PartitionSpec as P

INNER = 256


def halves(table):
    high = np.asarray(table, np.float32).astype(jnp.bfloat16)
    low = (np.asarray(table, np.float64) - high.astype(np.float64)).astype(np.float32).astype(jnp.bfloat16)
    return high, low


def split(value):
    high = value.astype(jnp.bfloat16)
    return high, (value - high.astype(jnp.float32)).astype(jnp.bfloat16)


def tables(span):
    outer = span // INNER
    step_out = np.arange(outer, dtype=np.float64)
    step_in = np.arange(INNER, dtype=np.float64)
    angle = 2 * np.pi * np.mod((4 * step_out[:, None] + 1) * step_out[None, :], 4 * outer) / (4 * outer)
    cos_out, sin_out = np.cos(angle), -np.sin(angle)
    first = np.concatenate(halves(np.concatenate([cos_out, sin_out], axis=0)), axis=1)
    angle = 2 * np.pi * np.mod((4 * step_out[:, None] + 1) * step_in[None, :], 4 * span) / (4 * span)
    twiddle = np.stack([np.cos(angle), -np.sin(angle)]).astype(np.float32)
    angle = 2 * np.pi * np.mod(step_in[:, None] * step_in[None, :], INNER) / INNER
    cos_in, sin_in = np.cos(angle), -np.sin(angle)
    second = np.concatenate(halves(np.block([[cos_in, sin_in], [-sin_in, cos_in]])), axis=0)
    last = np.concatenate(halves(np.concatenate([cos_out.T, -sin_out.T], axis=1) / span), axis=1)
    return first, twiddle, second, last


def matmul(left, right):
    return jnp.dot(left, right, preferred_element_type=jnp.float32)


def table_left(table, value):
    high, low = split(value)
    depth = value.shape[0]
    return matmul(table[...], jnp.concatenate([high, high], axis=0)) + matmul(table[:, :depth], low)


def table_right(value, table):
    high, low = split(value)
    depth = value.shape[1]
    return matmul(jnp.concatenate([high, high], axis=1), table[...]) + matmul(low, table[:depth, :])


def conv_row(signal, response, first, twiddle, second, last):
    outer = signal.shape[0]
    mid = table_left(first, jnp.concatenate([signal, response], axis=1))
    tw_real, tw_imag = twiddle[0], twiddle[1]
    turned = []
    for place in range(2):
        cols = slice(place * INNER, (place + 1) * INNER)
        real, imag = mid[:outer, cols], mid[outer:, cols]
        turned.append(jnp.concatenate(
            [real * tw_real - imag * tw_imag, real * tw_imag + imag * tw_real], axis=1
        ))
    spectra = table_right(jnp.concatenate(turned, axis=0), second)
    s_real, s_imag = spectra[:outer, :INNER], spectra[:outer, INNER:]
    r_real, r_imag = spectra[outer:, :INNER], spectra[outer:, INNER:]
    prod = jnp.concatenate(
        [s_real * r_real - s_imag * r_imag, -(s_real * r_imag + s_imag * r_real)], axis=1
    )
    back = table_right(prod, second)
    real, imag = back[:, :INNER], back[:, INNER:]
    turned = jnp.concatenate(
        [real * tw_real - imag * tw_imag, imag * tw_real + real * tw_imag], axis=0
    )
    return table_left(last, turned)


MESH_ID = pl.DeviceIdType.MESH
DEPTH = 1
LAG = 1


def partners(groups):
    return list(range(groups // 2, groups)) + list(range(1, groups // 2))


def flip(index, mask):
    bit = 1
    while bit <= mask:
        if mask & bit:
            index = index + bit - 2 * bit * ((index // bit) % 2)
        bit *= 2
    return index


def layer_kernel(
    groups, own_rows, chans, signal, response, gating, skip, weight,
    first, twiddle, second, last, out,
    send, held, made, conv, mixed, wall, wturn,
    fwd_send, fwd_recv, back_send, back_recv, own_sem, row_send, row_recv, w_send, w_recv, sib_sem, sib_recv, rel_send, rel_recv,
):
    chan_rows = groups * own_rows
    tiles_in = signal.shape[1]
    samples = tiles_in * 128
    pieces = samples // INNER
    chips = chans // 2
    me = lax.axis_index("seq")
    mine = lax.axis_index("chan")
    chip, core = mine // 2, mine % 2
    sibling = chip * 2 + 1 - core
    out_rows = out.shape[0]
    order = partners(groups)

    barrier = pltpu.get_barrier_semaphore()
    for mask in order:
        pl.semaphore_signal(barrier, inc=1, device_id={"seq": flip(me, mask)}, device_id_type=MESH_ID)
    for off in range(1, chans):
        pl.semaphore_signal(barrier, inc=1, device_id={"chan": lax.rem(mine + off, chans)}, device_id_type=MESH_ID)
    pl.semaphore_wait(barrier, groups + chans - 2)

    def forward(j, mask):
        return pltpu.make_async_remote_copy(
            send.at[j, flip(me, mask)], held.at[j, me], fwd_send.at[j, mask - 1], fwd_recv.at[j, mask - 1],
            device_id={"seq": flip(me, mask)}, device_id_type=MESH_ID)

    def arrived(j, who):
        size = 2 * pieces
        return conv.at[pl.ds(pl.multiple_of((j * groups + who) * size, size), size), :]

    def leaving(j, who):
        size = 2 * pieces
        return made.at[pl.ds(pl.multiple_of((j * groups + who) * size, size), size), :]

    def backward(j, mask):
        return pltpu.make_async_remote_copy(
            leaving(j, flip(me, mask)), arrived(j, me), back_send.at[j, mask - 1], back_recv.at[j, mask - 1],
            device_id={"seq": flip(me, mask)}, device_id_type=MESH_ID)

    def own_in(j):
        return pltpu.make_async_copy(send.at[j, me], held.at[j, me], own_sem.at[0, j])

    def own_back(j):
        return pltpu.make_async_copy(leaving(j, me), arrived(j, me), own_sem.at[1, j])

    bands = groups // 8

    def chunk(who, j):
        return mixed.at[pl.ds((who * own_rows + j) * bands, bands)]

    def to_sibling(j):
        return pltpu.make_async_remote_copy(
            chunk(mine, j), chunk(mine, j), sib_sem.at[j], sib_recv.at[j],
            device_id={"chan": sibling}, device_id_type=MESH_ID)

    def to_chip(j, off):
        return pltpu.make_async_remote_copy(
            chunk(mine, j), chunk(mine, j), row_send.at[j, off - 1], row_recv.at[j, off - 1],
            device_id={"chan": lax.rem(chip + off, chips) * 2 + core}, device_id_type=MESH_ID)

    def relay(j, off):
        who = lax.rem(chip + chips - off, chips) * 2 + core
        return pltpu.make_async_remote_copy(
            chunk(who, j), chunk(who, j), rel_send.at[j, off - 1], rel_recv.at[j, off - 1],
            device_id={"chan": sibling}, device_id_type=MESH_ID)

    own_weights = wall.at[pl.ds(pl.multiple_of(mine * chan_rows, 8), chan_rows), :]

    def weights(off):
        return pltpu.make_async_remote_copy(
            weight, own_weights, w_send.at[off - 1], w_recv.at[off - 1],
            device_id={"chan": lax.rem(mine + off, chans)}, device_id_type=MESH_ID)

    def launch(j):
        for g in range(groups):
            row = j * groups + g
            band, lane_row = row // 8, g % 8
            for place, ref in enumerate((signal, response)):
                for half in range(2):
                    send[j, g, place, :, half * 128:(half + 1) * 128] = ref[
                        band, pl.ds(half, pieces, stride=2), lane_row, :
                    ]
        for mask in order:
            forward(j, mask).start()
        own_in(j).start()

    def convolve(j):
        own_in(j).wait()
        for mask in order:
            forward(j, mask).wait_recv()
        rows = held[j]
        result = conv_row(
            rows[:, 0].reshape(groups * pieces, INNER), rows[:, 1].reshape(groups * pieces, INNER),
            first, twiddle, second, last,
        )
        for g in range(groups):
            for half in range(2):
                start = pl.multiple_of(((j * groups + g) * 2 + half) * pieces, pieces)
                made[pl.ds(start, pieces), :] = result[g * pieces:(g + 1) * pieces, half * 128:(half + 1) * 128]
        for mask in order:
            backward(j, mask).start()
        own_back(j).start()

    def gate(j):
        own_back(j).wait()
        for mask in order:
            backward(j, mask).wait_recv()
        for band in range(bands):
            here = j * bands + band
            gain = skip[pl.ds(pl.multiple_of(here * 8, 8), 8), :]
            for tile in range(tiles_in):
                start = (j * groups + band * 8) * 2 * pieces + (tile % 2) * pieces + tile // 2
                mixed[mine * own_rows * bands + here, tile] = gating[here, tile] * (
                    conv[pl.ds(start, 8, stride=2 * pieces), :] + gain * signal[here, tile]
                )
        to_sibling(j).start()
        for off in range(1, chips):
            to_chip(j, off).start()

    def pass_on(j):
        for off in range(1, chips):
            to_chip(j, off).wait_recv()
            relay(j, off).start()

    for j in range(min(DEPTH, own_rows)):
        launch(j)
    for off in range(1, chans):
        weights(off).start()
    wall[pl.ds(pl.multiple_of(mine * chan_rows, 8), chan_rows), :] = weight[...]

    @pl.loop(0, own_rows + LAG + 1)
    def _(t):
        @pl.when(t < own_rows)
        def _():
            for mask in order:
                forward(t, mask).wait_send()

            @pl.when(t + DEPTH < own_rows)
            def _():
                launch(t + DEPTH)

            convolve(t)

        @pl.when((t >= LAG) & (t < own_rows + LAG))
        def _():
            gate(t - LAG)

        @pl.when(t >= LAG + 1)
        def _():
            pass_on(t - LAG - 1)

    for off in range(1, chans):
        weights(off).wait()
    wturn[...] = jnp.transpose(wall[...])
    w_high, w_low = split(wturn[pl.ds(pl.multiple_of(mine * out_rows, 8), out_rows), :])
    w_both = jnp.concatenate([w_high, w_low], axis=0)

    @pl.loop(0, own_rows)
    def _(j):
        for mask in order:
            backward(j, mask).wait_send()
        to_sibling(j).wait()
        for off in range(1, chips):
            to_chip(j, off).wait_send()
            relay(j, off).wait()

    depth = chans * chan_rows

    @pl.loop(0, pieces)
    def _(i):
        data = jnp.concatenate([mixed[:, 2 * i + half].reshape(depth, 128) for half in range(2)], axis=1)
        high, low = split(data)
        both = matmul(w_both, high)
        out[:, pl.ds(pl.multiple_of(i * INNER, INNER), INNER)] = (
            both[:out_rows] + both[out_rows:] + matmul(w_high, low)
        )


def tiles(value):
    rows, columns = value.shape
    return value.reshape(rows // 8, 8, columns // 128, 128).transpose(0, 2, 1, 3)


def per_device(signal, gating, response, skip_gain, mixing_weight):
    chan_rows, samples = signal.shape
    groups = lax.axis_size("seq")
    chans = lax.axis_size("chan")
    own_rows = chan_rows // groups
    pieces = samples // INNER
    chips = chans // 2
    depth = mixing_weight.shape[0]
    out_rows = depth // chans
    consts = [jnp.asarray(t) for t in tables(groups * samples)]
    skip = jnp.broadcast_to(skip_gain[:, None], (chan_rows, 128))
    whole = pl.BlockSpec(memory_space=pltpu.VMEM)
    f32 = jnp.float32
    sems = pltpu.SemaphoreType.DMA
    return pl.pallas_call(
        partial(layer_kernel, groups, own_rows, chans),
        in_specs=[whole] * 9,
        out_specs=whole,
        out_shape=jax.ShapeDtypeStruct((out_rows, samples), f32),
        scratch_shapes=[
            pltpu.VMEM((own_rows, groups, 2, pieces, INNER), f32),
            pltpu.VMEM((own_rows, groups, 2, pieces, INNER), f32),
            pltpu.VMEM((chan_rows * 2 * pieces, 128), f32),
            pltpu.VMEM((chan_rows * 2 * pieces, 128), f32),
            pltpu.VMEM((chans * chan_rows // 8, samples // 128, 8, 128), f32),
            pltpu.VMEM((chans * chan_rows, depth), f32),
            pltpu.VMEM((depth, chans * chan_rows), f32),
            sems((own_rows, groups - 1)), sems((own_rows, groups - 1)),
            sems((own_rows, groups - 1)), sems((own_rows, groups - 1)),
            sems((2, own_rows)),
            sems((own_rows, chips - 1)), sems((own_rows, chips - 1)),
            sems((chans - 1,)), sems((chans - 1,)),
            sems((own_rows,)), sems((own_rows,)),
            sems((own_rows, chips - 1)), sems((own_rows, chips - 1)),
        ],
        compiler_params=pltpu.CompilerParams(
            collective_id=0, has_side_effects=True, vmem_limit_bytes=62 * 2**20
        ),
        name="layer",
    )(tiles(signal), tiles(response), tiles(gating), skip, mixing_weight.T, *consts)


def solution(mesh):
    in_specs = (P("chan", "seq"), P("chan", "seq"), P("chan", "seq"), P("chan"), P(None, "chan"))
    out_specs = P("chan", "seq")
    return jax.shard_map(
        per_device, mesh=mesh, in_specs=in_specs, out_specs=out_specs, check_vma=False
    )
```
